512 devices in a mesh: grp: 16 (over z), tp: 32 (over y, x, core).
Axes of the slice: x: 4, y: 4, z: 16, core: 2. Of those that a mesh axis runs over, the one named last changes fastest.
Arguments:
- attention_output: bfloat16 [512, 8192], P('grp', 'tp'), may hold values from -6 to 6
- output_projection: bfloat16 [8192, 8192], P('tp', 'grp'), may hold values from -0.0625 to 0.0625
- adapter_down_weight: bfloat16 [256, 8192, 64], P('grp', 'tp'), may hold values from -0.0625 to 0.0625
- adapter_up_weight: bfloat16 [256, 64, 8192], P('tp', None, 'grp'), may hold values from -0.75 to 0.75
- residual: bfloat16 [512, 8192], P('tp', 'grp')
- final_norm_gain: bfloat16 [8192], P('grp'), may hold values from 0.5 to 1.5
- vocab_head_weight: bfloat16 [8192, 65536], P('grp', 'tp')
- row_adapter_index: int32 [512], replicated, may hold values from 0 to 255, as said below
- row_grammar_state: int32 [512], replicated, may hold values from 0 to 39
- grammar_token_bits: int32 [40, 2048], P(None, 'tp'), may hold values from -2147483647 to 2147483647, as said below
Outputs:
- log_probs: float32 [512, 65536], P('grp', 'tp')
The draws below stay inside these ranges and needn't reach their ends.
Inputs may be any that keep to these rules, and one draw needn't show every extreme that they name: `row_adapter_index`: no adapter is named by more than 4 rows; at least one is named by exactly 4. `grammar_token_bits`: the lowest bit of every word is set.
All inputs are finite; a program needn't handle non-finite values.
Results may differ from the reference program's by a relative error of at most 0.00105.
The reference program's roundings to bfloat16 on the way (of `latent`, `layer_out` and `scaled`) count: a program that leaves them out, or rounds other values in their place, can miss the bound.
Values may be sent and summed in bfloat16 or wider, within the bound.
No kernel may reach another device: no remote copies, remote signals or barrier semaphores. Data moves between devices by JAX's collectives and lax.ppermute only.
A program may use at most 64 MiB of HBM per device.

```python
import math
import jax
import jax.numpy as jnp
from jax import lax

MODEL_WIDTH = 8192
VOCAB = 65536
ADAPTER_RANK = 64
SCHEMAS = 40
MOST = 4
ROWS = 512
ADAPTER_TOTAL = 256


def draw_row_adapter_index(key, part):
    heat_key, jitter_key, hot_key, order_key = jax.random.split(key, 4)
    slot_count = ADAPTER_TOTAL * MOST
    slot_index = jnp.arange(slot_count, dtype=jnp.int32)
    owners = slot_index // MOST
    heat_level = jax.random.randint(heat_key, (ADAPTER_TOTAL,), 0, 4, dtype=jnp.int32)
    jitter_draw = jax.random.randint(jitter_key, (slot_count,), 0, 4096, dtype=jnp.int32)
    hottest = jax.random.randint(hot_key, (), 0, ADAPTER_TOTAL, dtype=jnp.int32)
    scores = jitter_draw + heat_level[owners] * 2048 + jnp.where(owners == hottest, 16384, 0)
    scores = scores + jnp.where(slot_index == slot_count - MOST, 12000, 0)
    scores = scores * slot_count + slot_index
    picked = lax.top_k(scores, ROWS)[1]
    chosen = owners[picked]
    shuffle = jax.random.permutation(order_key, ROWS)
    return chosen[shuffle].astype(jnp.int32)


def draw_grammar_token_bits(key, part):
    packed = jax.random.randint(key, (SCHEMAS, VOCAB // 32), -2147483648, 2147483647, dtype=jnp.int32)
    return jnp.bitwise_or(packed, 1)


def draw_residual(key, part):
    base_key = jax.random.fold_in(key, 0)
    position = jnp.arange(MODEL_WIDTH, dtype=jnp.float32) / MODEL_WIDTH
    values = jax.random.normal(base_key, (ROWS, MODEL_WIDTH), jnp.float32)
    columns = 1.5 * 3.0 ** position
    return (values * columns[None, :]).astype(jnp.bfloat16)


def draw_vocab_head_weight(key, part):
    base_key = jax.random.fold_in(key, 0)
    position = jnp.arange(VOCAB, dtype=jnp.float32) / VOCAB
    rising = 1.0 + 0.12 * position
    values = jax.random.normal(base_key, (MODEL_WIDTH, VOCAB), jnp.float32) * (3.0 / math.sqrt(MODEL_WIDTH)) * rising[None, :]
    return values.astype(jnp.bfloat16)


def set_ends(drawn, own_key, low, largest):
    longest = drawn.shape.index(max(drawn.shape))
    spots = []
    for shift in (0, 1):
        where = [jax.random.randint(jax.random.fold_in(own_key, axis), (), 0, length) for axis, length in enumerate(drawn.shape)]
        where[longest] = (where[longest] + shift) % drawn.shape[longest]
        spots.append(tuple(where))
    return drawn.at[spots[0]].set(low).at[spots[1]].set(largest)


def steps_of(key, dims, shards, smallest, largest):
    gain, own = 1.0, jax.random.fold_in(key, 6)
    for dim, blocks in shards:
        steps = jnp.exp(jax.random.uniform(jax.random.fold_in(own, dim), (blocks,), jnp.float32, smallest / len(shards), largest / len(shards)))
        gain = gain * jnp.repeat(steps, dims[dim] // blocks).reshape([-1 if axis == dim else 1 for axis in range(len(dims))])
    return gain


def centred(rng, dims, spread, bound, pieces=(), held_as=jnp.bfloat16):
    array = spread * jax.random.normal(rng, dims, jnp.float32)
    if pieces:
        array = array * steps_of(rng, dims, pieces, -0.22, 0.18)
    return jnp.clip(array, -bound, bound).astype(held_as)


def setup_inputs(seed: int = 0) -> dict:
    key_list = jax.random.split(jax.random.key(seed), 11)
    return {
        "attention_output": centred(key_list[0], (ROWS, MODEL_WIDTH), 1.0, 6.0, ((0, 16), (1, 32))),
        "output_projection": centred(key_list[1], (MODEL_WIDTH, MODEL_WIDTH), MODEL_WIDTH ** -0.5, 0.0625, ((0, 32), (1, 16))),
        "adapter_down_weight": centred(key_list[2], (ADAPTER_TOTAL, MODEL_WIDTH, ADAPTER_RANK), MODEL_WIDTH ** -0.5, 0.0625, ((0, 16), (1, 32))),
        "adapter_up_weight": centred(key_list[3], (ADAPTER_TOTAL, ADAPTER_RANK, MODEL_WIDTH), ADAPTER_RANK ** -0.5, 0.75, ((0, 32), (2, 16))),
        "residual": draw_residual(jax.random.fold_in(key_list[10], 71), 0),
        "final_norm_gain": jnp.clip(1.0 + 0.1 * jax.random.normal(key_list[5], (MODEL_WIDTH,), jnp.float32), 0.5, 1.5).astype(jnp.bfloat16),
        "vocab_head_weight": draw_vocab_head_weight(jax.random.fold_in(key_list[10], 71), 0),
        "row_adapter_index": draw_row_adapter_index(jax.random.fold_in(key_list[10], 71), 0),
        "row_grammar_state": set_ends(jax.random.randint(key_list[8], (ROWS,), 0, SCHEMAS), jax.random.fold_in(key_list[8], 1), 0, SCHEMAS - 1).astype(jnp.int32),
        "grammar_token_bits": draw_grammar_token_bits(jax.random.fold_in(key_list[10], 71), 0),
    }


EPSILON = 1e-05

def unpack_bits(packed):
    shifts = jnp.arange(32, dtype=jnp.int32)
    bits_out = jnp.bitwise_and(jnp.right_shift(packed[:, :, None], shifts[None, None, :]), 1)
    return bits_out.reshape(packed.shape[0], packed.shape[1] * 32)

def reference(attention_output, output_projection, adapter_down_weight, adapter_up_weight, residual, final_norm_gain, vocab_head_weight, row_adapter_index, row_grammar_state, grammar_token_bits):
    base_out = jnp.dot(attention_output, output_projection, preferred_element_type=jnp.float32)

    def adapt_row(row_item):
        row_vector, adapter_number = row_item
        shrink_matrix = lax.dynamic_index_in_dim(adapter_down_weight, adapter_number, 0, keepdims=False)
        latent = jnp.dot(row_vector[None, :], shrink_matrix, preferred_element_type=jnp.float32).astype(jnp.bfloat16)
        expand_matrix = lax.dynamic_index_in_dim(adapter_up_weight, adapter_number, 0, keepdims=False)
        return jnp.dot(latent, expand_matrix, preferred_element_type=jnp.float32)[0]
    delta_out = lax.map(adapt_row, (attention_output, row_adapter_index))
    layer_out = (residual.astype(jnp.float32) + base_out + delta_out).astype(jnp.bfloat16)
    layer_float = layer_out.astype(jnp.float32)
    squares = lax.optimization_barrier(jnp.sum(layer_float * layer_float, axis=1))
    factor = lax.rsqrt(squares / MODEL_WIDTH + EPSILON)
    scaled = (layer_float * final_norm_gain.astype(jnp.float32)[None, :]).astype(jnp.bfloat16)
    logits = jnp.dot(scaled, vocab_head_weight, preferred_element_type=jnp.float32) * factor[:, None]
    mask_table = unpack_bits(grammar_token_bits) > 0
    allowed = mask_table[row_grammar_state]
    masked = jnp.where(allowed, logits, -jnp.inf)
    highest = lax.optimization_barrier(jnp.max(masked, axis=1))
    summed = lax.optimization_barrier(jnp.sum(jnp.exp(masked - highest[:, None]), axis=1))
    return jnp.where(allowed, logits - highest[:, None] - jnp.log(summed)[:, None], 0.0)
```

```python
import jax
import jax.numpy as jnp
from jax import lax
from jax.sharding import PartitionSpec as P

MODEL_WIDTH = 8192
MOST = 4


EPSILON = 1e-05


TP_Y = 4
TP_XC = 8
ACROSS_Y = [[TP_XC * y + k for y in range(TP_Y)] for k in range(TP_XC)]
ACROSS_XC = [[TP_XC * y + k for k in range(TP_XC)] for y in range(TP_Y)]


def exchange(blocks, axis, groups=None):
    return lax.all_to_all(blocks, axis, 0, 0, tiled=True, axis_index_groups=groups)


def gathered(value, axis, count, groups=None):
    return exchange(jnp.broadcast_to(value[None], (count,) + value.shape), axis, groups)


def slot_table(row_adapter_index, adapter_count):
    numbers = jnp.arange(adapter_count, dtype=jnp.int32)
    matches = (row_adapter_index[None, :] == numbers[:, None]).astype(jnp.int32)
    places = jnp.cumsum(matches, axis=1) - 1
    heat_tiers = jnp.arange(MOST, dtype=jnp.int32)
    return (matches[:, None, :] == 1) & (places[:, None, :] == heat_tiers[None, :, None])


def unpack_bits(packed):
    shifts = jnp.arange(32, dtype=jnp.int32)
    bits_out = jnp.bitwise_and(jnp.right_shift(packed[:, :, None], shifts[None, None, :]), 1)
    return bits_out.reshape(packed.shape[0], packed.shape[1] * 32).astype(jnp.float32)


def row_masks(mask_table, states):
    onehot_rows = (
        states[:, None] == jnp.arange(mask_table.shape[0], dtype=jnp.int32)[None, :]
    ).astype(jnp.float32)
    return jnp.dot(onehot_rows, mask_table, precision=lax.Precision.HIGHEST) > 0.5


def softmax_parts(logits, allowed):
    masked = jnp.where(allowed, logits, -jnp.inf)
    highest = jnp.max(masked, axis=1)
    summed = jnp.sum(jnp.exp(masked - highest[:, None]), axis=1)
    return (highest, summed)


def body(
    attention_output,
    output_projection,
    adapter_down_weight,
    adapter_up_weight,
    residual,
    final_norm_gain,
    vocab_head_weight,
    row_adapter_index,
    row_grammar_state,
    grammar_token_bits,
):
    grp_index = lax.axis_index("grp")
    tp_index = lax.axis_index("tp")
    grp_size, tp_size = lax.axis_size("grp"), lax.axis_size("tp")
    features = attention_output.shape[1]
    all_rows = gathered(attention_output, "grp", grp_size).reshape(-1, features)
    row_total = all_rows.shape[0]
    per_group = adapter_down_weight.shape[0]
    rank = adapter_down_weight.shape[2]
    per_tensor_part = adapter_up_weight.shape[0]
    adapter_count = per_tensor_part * tp_size
    slot_mask = slot_table(row_adapter_index, adapter_count)
    down_select = lax.dynamic_slice_in_dim(slot_mask, grp_index * per_group, per_group, 0).astype(
        jnp.bfloat16
    )
    slot_row_list = jnp.einsum(
        "amr,rf->amf", down_select, all_rows, preferred_element_type=jnp.float32
    ).astype(jnp.bfloat16)
    partial_latent = jnp.einsum(
        "cse,ceu->csu", slot_row_list, adapter_down_weight, preferred_element_type=jnp.float32
    ).astype(jnp.bfloat16)
    packed = partial_latent.reshape(per_group * MOST * rank // 128, 128)
    partial_all = gathered(packed, "grp", grp_size)
    shares = exchange(partial_all.reshape(tp_size, -1, 128), "tp")
    local_latent = (
        jnp.sum(shares.astype(jnp.float32), axis=0)
        .astype(jnp.bfloat16)
        .reshape(per_tensor_part, MOST, rank)
    )
    slot_delta = jnp.einsum(
        "tsl,tlx->tsx", local_latent, adapter_up_weight, preferred_element_type=jnp.float32
    )
    up_select = lax.dynamic_slice_in_dim(
        slot_mask, tp_index * per_tensor_part, per_tensor_part, 0
    ).astype(jnp.float32)
    delta_rows = jnp.einsum("amr,amf->rf", up_select, slot_delta, precision=lax.Precision.HIGHEST)
    term_sum = jnp.dot(all_rows, output_projection, preferred_element_type=jnp.float32) + delta_rows
    width = term_sum.shape[1]
    own_rows = residual.shape[0]
    from_y = exchange(term_sum.astype(jnp.bfloat16).reshape(TP_Y, -1, width), "tp", ACROSS_Y)
    y_sum = jnp.sum(from_y.astype(jnp.float32), axis=0)
    from_xc = exchange(
        y_sum.astype(jnp.bfloat16).reshape(TP_XC, own_rows, width), "tp", ACROSS_XC
    )
    own_out = (
        jnp.sum(from_xc.astype(jnp.float32), axis=0) + residual.astype(jnp.float32)
    ).astype(jnp.bfloat16)
    strip = gathered(own_out, "tp", TP_XC, ACROSS_XC).reshape(-1, width)
    layer_out = gathered(strip, "tp", TP_Y, ACROSS_Y).reshape(row_total, width)
    layer_float = layer_out.astype(jnp.float32)
    square_part = jnp.sum(layer_float * layer_float, axis=1)
    scaled = (layer_float * final_norm_gain.astype(jnp.float32)[None, :]).astype(jnp.bfloat16)
    logit_part = jnp.dot(scaled, vocab_head_weight, preferred_element_type=jnp.float32)
    logit_rows, squares = (
        lax.psum_scatter(logit_part, "grp", scatter_dimension=0, tiled=True),
        lax.psum_scatter(square_part, "grp", scatter_dimension=0, tiled=True),
    )
    factor = lax.rsqrt(squares / MODEL_WIDTH + EPSILON)
    own_count = logit_rows.shape[0]
    states = lax.dynamic_slice_in_dim(row_grammar_state, grp_index * own_count, own_count, 0)
    allowed = lax.optimization_barrier(row_masks(unpack_bits(grammar_token_bits), states))
    logits = logit_rows * factor[:, None]
    stats = jnp.stack(softmax_parts(logits, allowed))
    everyone = gathered(stats, "tp", tp_size)
    highest = jnp.max(everyone[:, 0], axis=0)
    summed = jnp.sum(everyone[:, 1] * jnp.exp(everyone[:, 0] - highest[None]), axis=0)
    return jnp.where(allowed, logits - highest[:, None] - jnp.log(summed)[:, None], 0.0)


def solution(mesh):
    in_specs = (
        P("grp", "tp"),
        P("tp", "grp"),
        P("grp", "tp", None),
        P("tp", None, "grp"),
        P("tp", "grp"),
        P("grp"),
        P("grp", "tp"),
        P(),
        P(),
        P(None, "tp"),
    )
    out_specs = P("grp", "tp")
    return jax.shard_map(body, mesh=mesh, in_specs=in_specs, out_specs=out_specs, check_vma=False)
```
